32 devices in a mesh: groups: 2 (over x), tm: 8 (over z, y), tile: 2 (over core).
Axes of the slice: x: 2, y: 2, z: 4, core: 2. Of those that a mesh axis runs over, the one named last changes fastest.
Arguments:
- activations: bfloat16 [64, 24, 16, 16, 128], P(('groups', 'tm'), 'tile'), parts along dimension 0, may hold values from -240 to 240
- tile_ids: int32 [48], P(('groups', 'tile')), parts along dimension 0, may hold values from 0 to 15, as said below
- tile_counts: int32 [4], P(('groups', 'tile')), parts along dimension 0, may hold values from 0 to 12, as said below
- first_gain: float32 [128], replicated, may hold values from 0.25 to 1.75
- first_shift: float32 [128], replicated, may hold values from -3 to 3
- first_conv: bfloat16 [3, 3, 3, 128, 128], replicated, may hold values from -0.109375 to 0.109375
- first_down: bfloat16 [3, 3, 3, 128, 128], replicated, may hold values from -0.109375 to 0.109375
- second_gain: float32 [128], replicated, may hold values from 0.25 to 1.75
- second_shift: float32 [128], replicated, may hold values from -3 to 3
- second_conv: bfloat16 [3, 3, 3, 128, 256], replicated, may hold values from -0.109375 to 0.109375
- second_short: bfloat16 [128, 256], replicated, may hold values from -0.5 to 0.5
- second_down: bfloat16 [3, 3, 3, 256, 256], replicated, may hold values from -0.078125 to 0.078125
Outputs:
- latents: bfloat16 [16, 16, 4, 4, 256], P(('groups', 'tm'), 'tile'), parts along dimension 0
The draws below stay inside these ranges and needn't reach their ends.
There are 2 independent parts, one for each index of `groups`. The reference program is written for one: setup_inputs(seed, part) draws one part's arguments, and reference() takes and returns one part's arrays. A program takes and returns all parts, laid end to end along the dimension named above; an argument that names none is the same for every part. Nothing has to cross between parts.
Inputs may be any that keep to these rules, and one draw needn't show every extreme that they name: `tile_ids`: slot j belongs to tile device j // 12. The live slots of the two devices hold distinct tiles; tiles d * 8 to (d + 1) * 8 - 1 are owned by tile device d. Slots that are not live hold arbitrary tile numbers. The first tile_counts[d] slots of device d are live. One device holds exactly 12 live tiles, all 8 tiles of one owner among them; the other holds the remaining 4 tiles of the other owner or, for a clip of the lower resolution, none.
All inputs are finite; a program needn't handle non-finite values.
Results may differ from the reference program's by a relative error of at most 0.0066.
Values may be sent and summed in bfloat16 or wider, within the bound.
A program may use at most 64 MiB of HBM per device.

```python
import math
import jax
import jax.numpy as jnp
from jax import lax

C1 = 128
C2 = 256
GROUPS = 32
S = 16
OWN = 8
CAP = 12
TILES = 16
SLOTS = 24
FRAMES = 32


def draw_activations(key, part):
    subkeys = jax.random.split(jax.random.fold_in(key, 11), 5)
    full_shape = (FRAMES, SLOTS, S, S, C1)
    frame_pos = jnp.arange(FRAMES, dtype=jnp.float32) / (FRAMES - 1)
    frame_scale = jnp.exp(jax.random.uniform(subkeys[0], (FRAMES,), minval=math.log(0.3), maxval=math.log(3.0)))
    place_scale = jnp.exp(jax.random.uniform(subkeys[1], (S, S), minval=math.log(0.7), maxval=math.log(1.4)))
    channel_scale = jnp.exp(jax.random.uniform(subkeys[2], (C1,), minval=math.log(0.35), maxval=math.log(3.5)))
    offsets = jax.random.uniform(subkeys[3], (C1,), minval=-1.0, maxval=1.0)
    frame_scale = frame_scale * jnp.exp(frame_pos * math.log(3.0)) / 1.7
    noise_part = jnp.clip(jax.random.normal(subkeys[4], full_shape), -4.0, 4.0)
    scaled = noise_part * frame_scale[:, None, None, None, None] * place_scale[:, :, None] * channel_scale
    return (scaled + offsets * channel_scale).astype(jnp.bfloat16)


def tile_plan(key):
    subkeys = jax.random.split(jax.random.fold_in(key, 29), 6)
    heavy_dev = jax.random.randint(subkeys[0], (), 0, 2)
    low_res = jax.random.randint(subkeys[1], (), 0, 2)
    full_owner = jax.random.randint(subkeys[2], (), 0, 2)
    half_own = OWN // 2
    other_tiles = (1 - full_owner) * OWN + jax.random.permutation(subkeys[3], OWN)
    heavy_list = jnp.concatenate([full_owner * OWN + jnp.arange(OWN, dtype=jnp.int32), other_tiles[:half_own]])
    heavy_list = jax.random.permutation(subkeys[4], heavy_list)
    spare_ids = jax.random.randint(subkeys[5], (CAP - (OWN - half_own),), 0, TILES)
    light_list = jnp.concatenate([other_tiles[half_own:], spare_ids])
    light_count = (OWN - half_own) * (1 - low_res)
    tile_list = jnp.where(heavy_dev == 0, jnp.concatenate([heavy_list, light_list]), jnp.concatenate([light_list, heavy_list]))
    count_list = jnp.where(jnp.arange(2) == heavy_dev, CAP, light_count)
    return (tile_list.astype(jnp.int32), count_list.astype(jnp.int32))


def draw_tile_ids(key, part):
    return tile_plan(key)[0]


def draw_tile_counts(key, part):
    return tile_plan(key)[1]


def centred(rng, extent, deviation, reach, kind=jnp.bfloat16):
    return jnp.clip(deviation * jax.random.normal(rng, extent, jnp.float32), -reach, reach).astype(kind)


def setup_inputs(seed: int = 0, part: int = 0) -> dict:
    key_list = jax.random.split(jax.random.key(seed), 13)
    part_keys = jax.random.split(jax.random.fold_in(key_list[12], part), 13)
    activations = draw_activations(jax.random.fold_in(jax.random.fold_in(key_list[12], part), 71), part)
    tile_ids = draw_tile_ids(jax.random.fold_in(jax.random.fold_in(key_list[12], part), 71), part)
    tile_counts = draw_tile_counts(jax.random.fold_in(jax.random.fold_in(key_list[12], part), 71), part)
    first_gain = jnp.clip(1.0 + 0.15 * jax.random.normal(key_list[3], (C1,), jnp.float32), 0.25, 1.75)
    first_shift = centred(key_list[4], (C1,), 0.5, 3.0, jnp.float32)
    first_conv = centred(key_list[5], (3, 3, 3, C1, C1), (27 * C1) ** -0.5, 0.109375)
    first_down = centred(key_list[6], (3, 3, 3, C1, C1), (27 * C1) ** -0.5, 0.109375)
    second_gain = jnp.clip(1.0 + 0.15 * jax.random.normal(key_list[7], (C1,), jnp.float32), 0.25, 1.75)
    second_shift = centred(key_list[8], (C1,), 0.5, 3.0, jnp.float32)
    second_conv = centred(key_list[9], (3, 3, 3, C1, C2), (27 * C1) ** -0.5, 0.109375)
    second_short = centred(key_list[10], (C1, C2), C1 ** -0.5, 0.5)
    second_down = centred(key_list[11], (3, 3, 3, C2, C2), (27 * C2) ** -0.5, 0.078125)
    return dict(activations=activations, tile_ids=tile_ids, tile_counts=tile_counts, first_gain=first_gain, first_shift=first_shift, first_conv=first_conv, first_down=first_down, second_gain=second_gain, second_shift=second_shift, second_conv=second_conv, second_short=second_short, second_down=second_down)


epsilon = 1e-06

def causal_norm(inputs, norm_gain, norm_shift):
    frames = inputs.shape[0]
    tile_count = inputs.shape[1]
    tile_side = inputs.shape[2]
    per_group = inputs.shape[4] // GROUPS
    values = inputs.astype(jnp.float32).reshape(frames, tile_count, tile_side * tile_side, GROUPS, per_group)
    total_sum = jnp.cumsum(lax.optimization_barrier(jnp.sum(values, axis=(2, 4))), axis=0)
    total_square = jnp.cumsum(lax.optimization_barrier(jnp.sum(values * values, axis=(2, 4))), axis=0)
    counts = (jnp.arange(frames, dtype=jnp.float32) + 1.0) * float(tile_side * tile_side * per_group)
    mean_value = total_sum / counts[:, None, None]
    spread = total_square / counts[:, None, None] - mean_value * mean_value
    inverse = lax.rsqrt(spread + epsilon)
    normed = (values - mean_value[:, :, None, :, None]) * inverse[:, :, None, :, None]
    normed = normed.reshape(inputs.shape) * norm_gain + norm_shift
    return jax.nn.silu(normed).astype(jnp.bfloat16)

def causal_conv(inputs, kernel, stride):
    leading = jnp.concatenate([inputs[:1], inputs[:1]], axis=0)
    padded = jnp.concatenate([leading, inputs], axis=0)
    return lax.conv_general_dilated(padded, kernel, (stride, stride, stride), ((0, 0), (1, 1), (1, 1)), dimension_numbers=('DNHWC', 'DHWIO', 'DNHWC'), preferred_element_type=jnp.float32)

def reference(activations, tile_ids, tile_counts, first_gain, first_shift, first_conv, first_down, second_gain, second_shift, second_conv, second_short, second_down):
    slot_index = jnp.arange(SLOTS, dtype=jnp.int32)
    slot_live = slot_index % CAP < tile_counts[slot_index // CAP]
    tile_index = jnp.arange(TILES, dtype=jnp.int32)
    select_int = ((tile_ids[None, :] == tile_index[:, None]) & slot_live[None, :]).astype(jnp.int32)
    tile_live = lax.optimization_barrier(jnp.sum(select_int, axis=1)) > 0
    source_slot = lax.optimization_barrier(jnp.sum(select_int * slot_index[None, :], axis=1)).astype(jnp.int32)
    tile_data = jnp.take(activations, source_slot, axis=1)
    tile_data = jnp.where(tile_live[None, :, None, None, None], tile_data, jnp.zeros_like(tile_data))
    first_hidden = causal_norm(tile_data, first_gain, first_shift)
    first_sum = (tile_data.astype(jnp.float32) + causal_conv(first_hidden, first_conv, 1)).astype(jnp.bfloat16)
    first_level = causal_conv(first_sum, first_down, 2).astype(jnp.bfloat16)
    second_hidden = causal_norm(first_level, second_gain, second_shift)
    shortcut = jnp.dot(first_level.reshape(-1, first_level.shape[4]), second_short, preferred_element_type=jnp.float32)
    shortcut = shortcut.reshape(first_level.shape[:4] + (second_short.shape[1],))
    second_sum = (causal_conv(second_hidden, second_conv, 1) + shortcut).astype(jnp.bfloat16)
    encoded = causal_conv(second_sum, second_down, 2)
    return jnp.where(tile_live[None, :, None, None, None], encoded, jnp.zeros_like(encoded)).astype(jnp.bfloat16)
```

```python
import functools

import jax
import jax.numpy as jnp
import numpy as np
from jax import lax
from jax.experimental import pallas as pl
from jax.experimental.pallas import tpu as pltpu
from jax.sharding import PartitionSpec as P

GROUPS = 32
OWN = 8
MOVED = 4
EPS = 1e-06
F32 = jnp.float32
BF16 = jnp.bfloat16
MESH = pl.DeviceIdType.MESH
VMEM = pl.BlockSpec(memory_space=pltpu.VMEM)
LIMIT = 56 << 20


def full(shape):
    return pl.BlockSpec(shape, lambda j, *_: (0,) * len(shape))


def prep_kernel(flag, own_ref, recv_ref, xa_ref, xb_ref, sums_ref):
    j = pl.program_id(0)
    keep = jnp.logical_or(j < OWN - MOVED, flag[0] == 1)

    def put(ref):
        for f in range(4):
            v = ref[f, 0]
            out = xa_ref if f < 2 else xb_ref
            out[f % 2, 0] = v
            w = v.astype(F32).reshape(256, 128)
            sums_ref[0, f, 0:1] = jnp.sum(w, axis=0, keepdims=True)
            sums_ref[0, f, 1:2] = jnp.sum(w * w, axis=0, keepdims=True)

    @pl.when(keep)
    def _():
        put(own_ref)

    @pl.when(jnp.logical_not(keep))
    def _():
        put(recv_ref)


def prep(acts, recv, flag):
    cells = acts.shape[2:]
    block = (4, 1) + cells
    pair = (2, 1) + cells
    return pl.pallas_call(
        prep_kernel,
        out_shape=(
            jax.ShapeDtypeStruct((2, OWN) + cells, BF16),
            jax.ShapeDtypeStruct((2, OWN) + cells, BF16),
            jax.ShapeDtypeStruct((OWN, 4, 2, 128), F32),
        ),
        grid_spec=pltpu.PrefetchScalarGridSpec(
            num_scalar_prefetch=1,
            grid=(OWN,),
            in_specs=[
                pl.BlockSpec(block, lambda j, f: (0, j, 0, 0, 0)),
                pl.BlockSpec(block, lambda j, f: (0, jnp.maximum(j - MOVED, 0), 0, 0, 0)),
            ],
            out_specs=[
                pl.BlockSpec(pair, lambda j, f: (0, j, 0, 0, 0)),
                pl.BlockSpec(pair, lambda j, f: (0, j, 0, 0, 0)),
                pl.BlockSpec((1, 4, 2, 128), lambda j, f: (j, 0, 0, 0)),
            ],
        ),
        name="prep",
        compiler_params=pltpu.CompilerParams(vmem_limit_bytes=LIMIT),
    )(flag, acts, recv)


def stats_kernel(n, frames, per_frame, s_ref, g_ref, out_ref, mine, got, send, recv):
    me = lax.axis_index("tm")
    barrier = pltpu.get_barrier_semaphore()
    for k in range(1, n):
        pl.semaphore_signal(barrier, inc=1, device_id={"tm": lax.rem(me + k, n)}, device_id_type=MESH)
    partial = s_ref[0]
    for f in range(1, frames - 1):
        partial = partial + s_ref[f]
    mine[1] = partial
    mine[0] = partial + s_ref[frames - 1]
    pl.semaphore_wait(barrier, n - 1)
    copies = []
    for k in range(1, n):
        src, dst = (mine, got.at[k]) if k == 1 else (mine.at[0], got.at[k, 0])
        c = pltpu.make_async_remote_copy(
            src_ref=src,
            dst_ref=dst,
            send_sem=send.at[k],
            recv_sem=recv.at[k],
            device_id={"tm": lax.rem(me + k, n)},
            device_id_type=MESH,
        )
        c.start()
        copies.append(c)
    rest = jnp.zeros_like(partial)
    for k in range(n - 1, 1, -1):
        copies[k - 1].wait()
        rest = rest + jnp.where(k <= me, got[k, 0], 0.0)
    copies[0].wait()
    before = rest + jnp.where(me >= 1, got[1, 0], 0.0)
    before2 = rest + jnp.where(me >= 1, got[1, 1], 0.0)
    rows = [before2, before]
    run = before
    for f in range(frames):
        run = run + s_ref[f]
        rows.append(run)
    ri = lax.broadcasted_iota(jnp.int32, (128, 128), 0) // (128 // GROUPS)
    ci = lax.broadcasted_iota(jnp.int32, (128, 128), 1) // (128 // GROUPS)
    same = jnp.where(ri == ci, 1.0, 0.0).astype(F32)
    start = (me * frames).astype(F32)
    made = []
    for i, r in enumerate(rows):
        count = jnp.maximum(start + float(i - 1), 1.0) * per_frame
        inv_count = jnp.full((1, 128), 1.0, F32) / (jnp.zeros((1, 128), F32) + count)
        g = jnp.dot(r, same, precision=lax.Precision.HIGHEST, preferred_element_type=F32)
        m = g[0:OWN] * inv_count
        var = g[OWN : 2 * OWN] * inv_count - m * m
        made.append((m, lax.rsqrt(var + EPS) * g_ref[...]))
    for i in range(frames + 2):
        m, s = made[i]
        if i < 2:
            m = jnp.where(me == 0, made[2][0], m)
            s = jnp.where(me == 0, made[2][1], s)
        out_ref[i, 0] = m
        out_ref[i, 1] = s


def stats(sums, gain, n, per_frame, cid):
    frames = sums.shape[0]
    return pl.pallas_call(
        functools.partial(stats_kernel, n, frames, per_frame),
        out_shape=jax.ShapeDtypeStruct((frames + 2, 2, OWN, 128), F32),
        in_specs=[VMEM, VMEM],
        out_specs=VMEM,
        scratch_shapes=[
            pltpu.VMEM((2, 2 * OWN, 128), F32),
            pltpu.VMEM((n, 2, 2 * OWN, 128), F32),
            pltpu.SemaphoreType.DMA((n,)),
            pltpu.SemaphoreType.DMA((n,)),
        ],
        name="stats" + str(cid),
        compiler_params=pltpu.CompilerParams(collective_id=cid, has_side_effects=True),
    )(sums, gain.reshape(1, 128))


def silu(u):
    return (0.5 * u) * (1.0 + jnp.tanh(0.5 * u))


def shifted(v, side):
    rows = v.shape[0]
    col = lax.broadcasted_iota(jnp.int32, v.shape, 0) % side
    left = jnp.where(col == 0, 0.0, pltpu.roll(v, 1, axis=0))
    right = jnp.where(col == side - 1, 0.0, pltpu.roll(v, rows - 1, axis=0))
    return left, right


def first_kernel(base, second, flag, *refs):
    xa_ref, xb_ref, p_ref, shift_ref, conv_ref, down_ref = refs[:6]
    if second:
        prev_ref, got_ref, level_ref, sums_ref = refs[6:10]
    else:
        own_ref, next_ref = refs[6:8]
    buf, w2, wd, sf, lhs = refs[-5:]
    j = pl.program_id(0)

    @pl.when(j == 0)
    def _():
        zero = jnp.zeros((128, 128), BF16)
        for q in range(4):
            for b in range(3):
                for c in range(3):
                    for e in range(2):
                        a = q - e
                        k = (q % 2) * 384 + c * 128
                        w2[(q // 2) * 3 + b, k : k + 128, e * 128 : e * 128 + 128] = (
                            conv_ref[a, b, c] if 0 <= a < 3 else zero
                        )
        for b in range(3):
            for c in range(3):
                wd[b, c * 128 : c * 128 + 128, 0:128] = down_ref[2, b, c]
                wd[b, 384 + c * 128 : 512 + c * 128, 0:128] = zero
                wd[b, c * 128 : c * 128 + 128, 128:256] = down_ref[0, b, c]
                wd[b, 384 + c * 128 : 512 + c * 128, 128:256] = down_ref[1, b, c]
        edge = jnp.zeros((16, 768), BF16)
        for p in range(2):
            buf[p, 0:16] = edge
            buf[p, 272:288] = edge

    for q in range(4):
        x = (xa_ref if q < 2 else xb_ref)[q % 2, 0].astype(F32).reshape(256, 128)
        if second and q < 2:
            x = jnp.where(flag[0] == 1, xb_ref[0, 0].astype(F32).reshape(256, 128), x)
        mean = p_ref[base + q, 0, pl.ds(j, 1), :]
        scale = p_ref[base + q, 1, pl.ds(j, 1), :]
        h = silu((x - mean) * scale + shift_ref[...])
        left, right = shifted(h, 16)
        k = (q % 2) * 384
        buf[q // 2, 16:272, k : k + 128] = left.astype(BF16)
        buf[q // 2, 16:272, k + 128 : k + 256] = h.astype(BF16)
        buf[q // 2, 16:272, k + 256 : k + 384] = right.astype(BF16)
    acc = jnp.zeros((256, 256), F32)
    for p in range(2):
        for b in range(3):
            acc = acc + jnp.dot(buf[p, b * 16 : b * 16 + 256, :], w2[p * 3 + b], preferred_element_type=F32)
    for e in range(2):
        x = xb_ref[e, 0].astype(F32).reshape(256, 128)
        sf[e] = (x + acc[:, e * 128 : e * 128 + 128]).astype(BF16).astype(F32)
    row = pl.multiple_of(j * 64, 64)
    col = lax.broadcasted_iota(jnp.int32, (128, 128), 0) % 8
    for e in range(2):
        even = sf[e, pl.ds(0, 128, stride=2), :]
        odd = sf[e, pl.ds(1, 128, stride=2), :]
        prev = jnp.where(col == 0, 0.0, pltpu.roll(odd, 1, axis=0))
        for c, v in enumerate((prev, even, odd)):
            v = v.reshape(8, 2, 8, 128)
            top, low = v[:, 0], v[:, 1]
            up = jnp.concatenate([jnp.zeros((1, 8, 128), F32), low[:7]], axis=0)
            k = e * 384 + c * 128
            for b, u in enumerate((up, top, low)):
                lhs[b, pl.ds(row, 64), k : k + 128] = u.reshape(64, 128).astype(BF16)

    @pl.when(j == OWN - 1)
    def _():
        out = jnp.zeros((512, 256), F32)
        for b in range(3):
            out = out + jnp.dot(lhs[b], wd[b], preferred_element_type=F32)
        if not second:
            own_ref[...] = out[:, 0:128]
            next_ref[...] = out[:, 128:256]
        else:
            sf0 = got_ref[...] + out[:, 0:128]
            got_ref[...] = sf0
            last = (prev_ref[...] + out[:, 128:256]).astype(BF16)
            level_ref[1] = last

            @pl.when(flag[0] == 1)
            def _():
                extra = got_ref[...]
                for b in range(3):
                    twice = jnp.concatenate([lhs[b, :, 0:384], lhs[b, :, 0:384]], axis=1)
                    extra = extra + jnp.dot(twice, wd[b, :, 128:256], preferred_element_type=F32)
                got_ref[...] = extra

            level_ref[0] = got_ref[...].astype(BF16)
            for f in range(2):
                v = level_ref[f].astype(F32).reshape(OWN, 64, 128)
                sums_ref[f, 0:OWN] = jnp.sum(v, axis=1)
                sums_ref[f, OWN : 2 * OWN] = jnp.sum(v * v, axis=1)


def first_pair(xa, xb, params, shift, conv, down, flag, prev=None, got=None):
    second = prev is not None
    cells = xa.shape[2:]
    pair = pl.BlockSpec((2, 1) + cells, lambda j, f: (0, j, 0, 0, 0))
    rows = OWN * 64
    in_specs = [pair, pair, full(params.shape), full((1, 128)), full(conv.shape), full(down.shape)]
    args = [xa, xb, params, shift.reshape(1, 128), conv, down]
    if second:
        in_specs += [full((rows, 128))] * 2
        args += [prev, got]
        outs = (jax.ShapeDtypeStruct((2, rows, 128), BF16), jax.ShapeDtypeStruct((2, 2 * OWN, 128), F32))
    else:
        outs = (jax.ShapeDtypeStruct((rows, 128), F32),) * 2
    return pl.pallas_call(
        functools.partial(first_kernel, 0 if second else 2, second),
        out_shape=outs,
        grid_spec=pltpu.PrefetchScalarGridSpec(
            num_scalar_prefetch=1,
            grid=(OWN,),
            in_specs=in_specs,
            out_specs=[full(o.shape) for o in outs],
            scratch_shapes=[
                pltpu.VMEM((2, 288, 768), BF16),
                pltpu.VMEM((6, 768, 256), BF16),
                pltpu.VMEM((3, 768, 256), BF16),
                pltpu.VMEM((2, 256, 128), F32),
                pltpu.VMEM((3, rows, 768), BF16),
            ],
        ),
        name="firstb" if second else "firsta",
        cost_estimate=pl.CostEstimate(flops=8 * 10**9, bytes_accessed=6 * 10**6, transcendentals=10**6),
        compiler_params=pltpu.CompilerParams(vmem_limit_bytes=LIMIT),
    )(flag, *args)


def second_kernel(flag, halo_ref, lev_ref, p_ref, shift_ref, conv_ref, short_ref, down_ref, pick_ref, own_ref, next_ref, lhs):
    for t in range(OWN):
        for q in range(4):
            lo, hi = t * 64, t * 64 + 64
            if q < 2:
                x = jnp.where(flag[0] == 1, lev_ref[0, lo:hi].astype(F32), halo_ref[q, lo:hi].astype(F32))
            else:
                x = lev_ref[q - 2, lo:hi].astype(F32)
            h = silu((x - p_ref[q, 0, t : t + 1, :]) * p_ref[q, 1, t : t + 1, :] + shift_ref[...])
            left, right = shifted(h, 8)
            zero = jnp.zeros((8, 128), F32)
            for c, v in enumerate((left, h, right)):
                for b, u in enumerate(
                    (jnp.concatenate([zero, v[:56]], axis=0), v, jnp.concatenate([v[8:], zero], axis=0))
                ):
                    k = (b * 3 + c) * 128
                    lhs[q, lo:hi, k : k + 128] = u.astype(BF16)
    level2 = []
    for f in range(2):
        acc = jnp.dot(lev_ref[f], short_ref[...], preferred_element_type=F32)
        for a in range(3):
            acc = acc + jnp.dot(lhs[f + a], conv_ref[a], preferred_element_type=F32)
        level2.append(acc.astype(BF16))
    own = jnp.zeros((128, 256), F32)
    nxt = jnp.zeros((128, 256), F32)
    first = []
    for i in range(9):
        pick = pick_ref[i * 128 : i * 128 + 128]
        s0 = jnp.dot(pick, level2[0], preferred_element_type=F32).astype(BF16)
        s1 = jnp.dot(pick, level2[1], preferred_element_type=F32).astype(BF16)
        own = own + jnp.dot(s0, down_ref[18 + i], preferred_element_type=F32)
        nxt = nxt + jnp.dot(s0, down_ref[i], preferred_element_type=F32)
        nxt = nxt + jnp.dot(s1, down_ref[9 + i], preferred_element_type=F32)
        lhs[0, i * 0 : 128, i * 128 : i * 128 + 128] = s0[:, 0:128]
        lhs[1, i * 0 : 128, i * 128 : i * 128 + 128] = s0[:, 128:256]
    own_ref[...] = own
    next_ref[...] = nxt

    @pl.when(flag[0] == 1)
    def _():
        extra = own_ref[...]
        for i in range(9):
            s0 = jnp.concatenate(
                [lhs[0, 0:128, i * 128 : i * 128 + 128], lhs[1, 0:128, i * 128 : i * 128 + 128]], axis=1
            )
            extra = extra + jnp.dot(s0, down_ref[i], preferred_element_type=F32)
            extra = extra + jnp.dot(s0, down_ref[9 + i], preferred_element_type=F32)
        own_ref[...] = extra


def pick_matrix():
    m = np.zeros((9, OWN, 4, 4, OWN, 8, 8), np.float32)
    for b in range(3):
        for c in range(3):
            for y in range(4):
                for x in range(4):
                    h, w = 2 * y + b - 1, 2 * x + c - 1
                    if 0 <= h < 8 and 0 <= w < 8:
                        for t in range(OWN):
                            m[b * 3 + c, t, y, x, t, h, w] = 1.0
    return m.reshape(9 * OWN * 16, OWN * 64)


def second_block(halo, level, params, shift, conv, short, down, flag):
    out = jax.ShapeDtypeStruct((OWN * 16, 256), F32)
    return pl.pallas_call(
        second_kernel,
        out_shape=(out, out),
        in_specs=[pl.BlockSpec(memory_space=pltpu.SMEM)] + [VMEM] * 8,
        out_specs=[VMEM, VMEM],
        scratch_shapes=[pltpu.VMEM((4, OWN * 64, 1152), BF16)],
        name="secondk",
        compiler_params=pltpu.CompilerParams(vmem_limit_bytes=LIMIT),
    )(
        flag,
        halo,
        level,
        params,
        shift.reshape(1, 128),
        conv.reshape(3, 1152, 256),
        short,
        down.reshape(27, 256, 256),
        jnp.asarray(pick_matrix(), BF16),
    )


def passed(value, axis):
    count = lax.axis_size(axis)
    return lax.ppermute(value, axis, [(i, i + 1) for i in range(count - 1)])


def swapped(value):
    return lax.ppermute(value, "tile", [(0, 1), (1, 0)])


def body(
    activations,
    tile_ids,
    tile_counts,
    first_gain,
    first_shift,
    first_conv,
    first_down,
    second_gain,
    second_shift,
    second_conv,
    second_short,
    second_down,
):
    n = lax.axis_size("tm")
    me = lax.axis_index("tile")
    start = (lax.axis_index("tm") == 0).astype(jnp.int32).reshape(1)
    cap = activations.shape[1]
    recv = swapped(activations[:, OWN:cap])
    info = jnp.concatenate([tile_ids, tile_counts])
    other = swapped(info)
    heavy = (tile_counts[0] == cap).astype(jnp.int32).reshape(1)

    def encoded_ids(a, b):
        slots = jnp.arange(cap)
        ids_a = jnp.where(slots < a[cap], a[:cap], -1)
        ids_b = jnp.where(slots < b[cap], b[:cap], -1)
        kept = jnp.where(a[cap] == cap, ids_a[OWN - MOVED : OWN], ids_b[OWN:])
        return jnp.concatenate([ids_a[: OWN - MOVED], kept])

    ids = jnp.concatenate([encoded_ids(info, other), encoded_ids(other, info)])

    xa, xb, sums = prep(activations, recv, heavy)
    halo = passed(xb, "tm")
    sums = sums.transpose(1, 2, 0, 3).reshape(4, 2 * OWN, 128)
    side = activations.shape[2]
    params = stats(sums, first_gain, n, float(side * side * (128 // GROUPS)), 0)
    own1, next1 = first_pair(xa, xb, params, first_shift, first_conv, first_down, start)
    got1 = passed(next1, "tm")
    level, sums2 = first_pair(halo, xa, params, first_shift, first_conv, first_down, start, own1, got1)
    halo2 = passed(level, "tm")
    params2 = stats(sums2, second_gain, n, float(side * side // 4 * (128 // GROUPS)), 1)
    own2, next2 = second_block(halo2, level, params2, second_shift, second_conv, second_short, second_down, start)
    enc = (own2 + passed(next2, "tm")).astype(BF16).reshape(OWN, 16 * 256)
    both = jnp.concatenate([enc, swapped(enc)], axis=0)
    select = (ids[None, :] == (me * OWN + jnp.arange(OWN))[:, None]).astype(BF16)
    latents = jnp.dot(select, both, preferred_element_type=F32).astype(BF16)
    return latents.reshape(1, OWN, 4, 4, 256)


def solution(mesh):
    placed = (
        P(("groups", "tm"), "tile", None, None, None),
        P(("groups", "tile")),
        P(("groups", "tile")),
    ) + (P(),) * 9
    return jax.shard_map(
        body,
        mesh=mesh,
        in_specs=placed,
        out_specs=P(("groups", "tm"), "tile", None, None, None),
        check_vma=False,
    )
```

```python
import functools

import jax
import jax.numpy as jnp
import numpy as np
from jax import lax
from jax.experimental import pallas as pl
from jax.experimental.pallas import tpu as pltpu
from jax.sharding import PartitionSpec as P

GROUPS = 32
OWN = 8
MOVED = 4
EPS = 1e-06
F32 = jnp.float32
BF16 = jnp.bfloat16
MESH = pl.DeviceIdType.MESH
VMEM = pl.BlockSpec(memory_space=pltpu.VMEM)
LIMIT = 56 << 20


def full(shape):
    return pl.BlockSpec(shape, lambda j, *_: (0,) * len(shape))


def prep_kernel(flag, own_ref, recv_ref, xa_ref, xb_ref, sums_ref):
    j = pl.program_id(0)
    keep = jnp.logical_or(j < OWN - MOVED, flag[0] == 1)

    def put(ref):
        for f in range(4):
            v = ref[f, 0]
            out = xa_ref if f < 2 else xb_ref
            out[f % 2, 0] = v
            w = v.astype(F32).reshape(256, 128)
            sums_ref[f, pl.ds(j, 1)] = jnp.sum(w, axis=0, keepdims=True)
            sums_ref[f, pl.ds(OWN + j, 1)] = jnp.sum(w * w, axis=0, keepdims=True)

    @pl.when(keep)
    def _():
        put(own_ref)

    @pl.when(jnp.logical_not(keep))
    def _():
        put(recv_ref)


def prep(acts, recv, flag):
    cells = acts.shape[2:]
    block = (4, 1) + cells
    pair = (2, 1) + cells
    return pl.pallas_call(
        prep_kernel,
        out_shape=(
            jax.ShapeDtypeStruct((2, OWN) + cells, BF16),
            jax.ShapeDtypeStruct((2, OWN) + cells, BF16),
            jax.ShapeDtypeStruct((4, 2 * OWN, 128), F32),
        ),
        grid_spec=pltpu.PrefetchScalarGridSpec(
            num_scalar_prefetch=1,
            grid=(OWN,),
            in_specs=[
                pl.BlockSpec(block, lambda j, f: (0, jnp.where(f[0] == 1, j, jnp.minimum(j, MOVED - 1)), 0, 0, 0)),
                pl.BlockSpec(block, lambda j, f: (0, jnp.where(f[0] == 1, 0, jnp.maximum(j - MOVED, 0)), 0, 0, 0)),
            ],
            out_specs=[
                pl.BlockSpec(pair, lambda j, f: (0, j, 0, 0, 0)),
                pl.BlockSpec(pair, lambda j, f: (0, j, 0, 0, 0)),
                full((4, 2 * OWN, 128)),
            ],
        ),
        name="prep",
        compiler_params=pltpu.CompilerParams(vmem_limit_bytes=LIMIT),
    )(flag, acts, recv)


def silu(u):
    return (0.5 * u) * (1.0 + jnp.tanh(0.5 * u))


def shifted(v, side):
    rows = v.shape[0]
    col = lax.broadcasted_iota(jnp.int32, v.shape, 0) % side
    left = jnp.where(col == 0, 0.0, pltpu.roll(v, 1, axis=0))
    right = jnp.where(col == side - 1, 0.0, pltpu.roll(v, rows - 1, axis=0))
    return left, right


def pick_matrix():
    m = np.zeros((9, OWN, 4, 4, OWN, 8, 8), np.float32)
    for b in range(3):
        for c in range(3):
            for y in range(4):
                for x in range(4):
                    h, w = 2 * y + b - 1, 2 * x + c - 1
                    if 0 <= h < 8 and 0 <= w < 8:
                        for t in range(OWN):
                            m[b * 3 + c, t, y, x, t, h, w] = 1.0
    return m.reshape(9 * OWN * 16, OWN * 64)


def main_kernel(
    n,
    per_frame,
    xa_ref,
    xb_ref,
    s_ref,
    gain1_ref,
    shift1_ref,
    conv1_ref,
    down1_ref,
    gain2_ref,
    shift2_ref,
    conv2_ref,
    short_ref,
    down2_ref,
    pick_ref,
    out_ref,
    mine1,
    got1,
    mine2,
    got2,
    p1,
    p2,
    halo,
    buf,
    w2,
    wd,
    sf,
    lhs,
    own1,
    next1,
    part1,
    level,
    lhalo,
    lhs2,
    own2,
    next2,
    part2,
    enc,
    renc,
    send1,
    recv1,
    send2,
    recv2,
    sems,
):
    me = lax.axis_index("tm")
    right = lax.rem(me + 1, n)
    partner = 1 - lax.axis_index("tile")
    barrier = pltpu.get_barrier_semaphore()
    for k in range(1, n):
        pl.semaphore_signal(barrier, inc=1, device_id={"tm": lax.rem(me + k, n)}, device_id_type=MESH)
    pl.semaphore_signal(barrier, inc=1, device_id={"tile": partner}, device_id_type=MESH)

    def to_right(src, dst, i):
        return pltpu.make_async_remote_copy(
            src_ref=src,
            dst_ref=dst,
            send_sem=sems.at[2 * i],
            recv_sem=sems.at[2 * i + 1],
            device_id={"tm": right},
            device_id_type=MESH,
        )

    def send(copy):
        @pl.when(me < n - 1)
        def _():
            copy.start()

    def sent(copy):
        @pl.when(me < n - 1)
        def _():
            copy.wait_send()

    def landed(copy):
        @pl.when(me > 0)
        def _():
            copy.wait_recv()

    def fill(sums, mine):
        partial = sums[0]
        for f in range(1, len(sums) - 1):
            partial = partial + sums[f]
        mine[1] = partial
        mine[0] = partial + sums[-1]

    def share(mine, got, send_sem, recv_sem):
        copies = []
        for k in range(1, n):
            src, dst = (mine, got.at[k]) if k == 1 else (mine.at[0], got.at[k, 0])
            c = pltpu.make_async_remote_copy(
                src_ref=src,
                dst_ref=dst,
                send_sem=send_sem.at[k],
                recv_sem=recv_sem.at[k],
                device_id={"tm": lax.rem(me + k, n)},
                device_id_type=MESH,
            )
            c.start()
            copies.append(c)
        return copies

    def norms(sums, copies, got, gain, size, out):
        frames = len(sums)
        rest = jnp.zeros_like(sums[0])
        for k in range(n - 1, 1, -1):
            copies[k - 1].wait()
            rest = rest + jnp.where(k <= me, got[k, 0], 0.0)
        copies[0].wait()
        before = rest + jnp.where(me >= 1, got[1, 0], 0.0)
        rows = [rest + jnp.where(me >= 1, got[1, 1], 0.0), before]
        run = before
        for f in range(frames):
            run = run + sums[f]
            rows.append(run)
        ri = lax.broadcasted_iota(jnp.int32, (128, 128), 0) // (128 // GROUPS)
        ci = lax.broadcasted_iota(jnp.int32, (128, 128), 1) // (128 // GROUPS)
        same = jnp.where(ri == ci, 1.0, 0.0).astype(F32)
        grouped = jnp.dot(
            jnp.concatenate(rows, axis=0), same, precision=lax.Precision.HIGHEST, preferred_element_type=F32
        )
        start = (me * frames).astype(F32)
        made = []
        for i in range(frames + 2):
            count = jnp.maximum(start + float(i - 1), 1.0) * size
            inv_count = jnp.full((1, 128), 1.0, F32) / (jnp.zeros((1, 128), F32) + count)
            g = grouped[i * 2 * OWN : (i + 1) * 2 * OWN]
            m = g[0:OWN] * inv_count
            var = g[OWN : 2 * OWN] * inv_count - m * m
            made.append((m, lax.rsqrt(var + EPS) * gain[...]))
        for i in range(frames + 2):
            for z in range(2):
                v = made[i][z]
                out[i, z] = jnp.where(me == 0, made[2][z], v) if i < 2 else v

    sums1 = [s_ref[f] for f in range(4)]
    fill(sums1, mine1)
    pl.semaphore_wait(barrier, n)
    copies1 = share(mine1, got1, send1, recv1)

    zero = jnp.zeros((128, 128), BF16)
    for q in range(4):
        for b in range(3):
            for c in range(3):
                for e in range(2):
                    a = q - e
                    k = (q % 2) * 384 + c * 128
                    w2[(q // 2) * 3 + b, k : k + 128, e * 128 : e * 128 + 128] = (
                        conv1_ref[a, b, c] if 0 <= a < 3 else zero
                    )
    for b in range(3):
        for c in range(3):
            wd[b, c * 128 : c * 128 + 128, 0:128] = down1_ref[2, b, c]
            wd[b, 384 + c * 128 : 512 + c * 128, 0:128] = zero
            wd[b, c * 128 : c * 128 + 128, 128:256] = down1_ref[0, b, c]
            wd[b, 384 + c * 128 : 512 + c * 128, 128:256] = down1_ref[1, b, c]
    edge = jnp.zeros((16, 768), BF16)
    for p in range(2):
        buf[p, 0:16] = edge
        buf[p, 272:288] = edge

    norms(sums1, copies1, got1, gain1_ref, per_frame, p1)
    halo_copy = to_right(xb_ref, halo, 0)
    send(halo_copy)

    def first_tiles(base, ra, rb):
        def step(j, _):
            for q in range(4):
                x = (ra if q < 2 else rb)[q % 2, j].astype(F32).reshape(256, 128)
                mean = p1[base + q, 0, pl.ds(j, 1), :]
                scale = p1[base + q, 1, pl.ds(j, 1), :]
                h = silu((x - mean) * scale + shift1_ref[...])
                left, right_ = shifted(h, 16)
                k = (q % 2) * 384
                buf[q // 2, 16:272, k : k + 128] = left.astype(BF16)
                buf[q // 2, 16:272, k + 128 : k + 256] = h.astype(BF16)
                buf[q // 2, 16:272, k + 256 : k + 384] = right_.astype(BF16)
            acc = jnp.zeros((256, 256), F32)
            for p in range(2):
                for b in range(3):
                    acc = acc + jnp.dot(
                        buf[p, b * 16 : b * 16 + 256, :], w2[p * 3 + b], preferred_element_type=F32
                    )
            for e in range(2):
                x = rb[e, j].astype(F32).reshape(256, 128)
                sf[e] = (x + acc[:, e * 128 : e * 128 + 128]).astype(BF16).astype(F32)
            row = pl.multiple_of(j * 64, 64)
            col = lax.broadcasted_iota(jnp.int32, (128, 128), 0) % 8
            for e in range(2):
                even = sf[e, pl.ds(0, 128, stride=2), :]
                odd = sf[e, pl.ds(1, 128, stride=2), :]
                prev = jnp.where(col == 0, 0.0, pltpu.roll(odd, 1, axis=0))
                for c, v in enumerate((prev, even, odd)):
                    v = v.reshape(8, 2, 8, 128)
                    top, low = v[:, 0], v[:, 1]
                    up = jnp.concatenate([jnp.zeros((1, 8, 128), F32), low[:7]], axis=0)
                    k = e * 384 + c * 128
                    for b, u in enumerate((up, top, low)):
                        lhs[b, pl.ds(row, 64), k : k + 128] = u.reshape(64, 128).astype(BF16)
            return 0

        lax.fori_loop(0, OWN, step, 0)
        out = jnp.zeros((512, 256), F32)
        for b in range(3):
            out = out + jnp.dot(lhs[b], wd[b], preferred_element_type=F32)
        return out

    out = first_tiles(2, xa_ref, xb_ref)
    own1[...] = out[:, 0:128]
    next1[...] = out[:, 128:256]
    part_copy = to_right(next1, part1, 1)
    send(part_copy)

    @pl.when(me == 0)
    def _():
        halo[0] = xa_ref[0]
        halo[1] = xa_ref[0]

    landed(halo_copy)
    out = first_tiles(0, halo, xa_ref)
    level[1] = (own1[...] + out[:, 128:256]).astype(BF16)
    own1[...] = out[:, 0:128]

    @pl.when(me == 0)
    def _():
        extra = jnp.zeros((512, 128), F32)
        for b in range(3):
            twice = jnp.concatenate([lhs[b, :, 0:384], lhs[b, :, 0:384]], axis=1)
            extra = extra + jnp.dot(twice, wd[b, :, 128:256], preferred_element_type=F32)
        part1[...] = extra

    landed(part_copy)
    level[0] = (own1[...] + part1[...]).astype(BF16)
    sent(halo_copy)
    sent(part_copy)

    sums2 = []
    for f in range(2):
        v = level[f].astype(F32).reshape(OWN, 64, 128)
        sums2.append(jnp.concatenate([jnp.sum(v, axis=1), jnp.sum(v * v, axis=1)], axis=0))
    fill(sums2, mine2)
    copies2 = share(mine2, got2, send2, recv2)
    lhalo_copy = to_right(level, lhalo, 2)
    send(lhalo_copy)

    @pl.when(me == 0)
    def _():
        lhalo[0] = level[0]
        lhalo[1] = level[0]

    norms(sums2, copies2, got2, gain2_ref, per_frame / 4, p2)

    def second_tiles(base, ref):
        def step(t, _):
            rows = pl.ds(pl.multiple_of(t * 64, 64), 64)
            for q in range(2):
                x = ref[q, rows, :].astype(F32)
                mean = p2[base + q, 0, pl.ds(t, 1), :]
                scale = p2[base + q, 1, pl.ds(t, 1), :]
                h = silu((x - mean) * scale + shift2_ref[...])
                left, right_ = shifted(h, 8)
                pad = jnp.zeros((8, 128), F32)
                for c, v in enumerate((left, h, right_)):
                    up = jnp.concatenate([pad, v[:56]], axis=0)
                    low = jnp.concatenate([v[8:], pad], axis=0)
                    for b, u in enumerate((up, v, low)):
                        k = (b * 3 + c) * 128
                        lhs2[base + q, rows, k : k + 128] = u.astype(BF16)
            return 0

        lax.fori_loop(0, OWN, step, 0)

    second_tiles(2, level)
    landed(lhalo_copy)
    second_tiles(0, lhalo)
    level2 = []
    for f in range(2):
        acc = jnp.dot(level[f], short_ref[...], preferred_element_type=F32)
        for a in range(3):
            acc = acc + jnp.dot(lhs2[f + a], conv2_ref[a], preferred_element_type=F32)
        level2.append(acc.astype(BF16))
    own = jnp.zeros((128, 256), F32)
    nxt = jnp.zeros((128, 256), F32)
    for i in range(9):
        pick = pick_ref[i * 128 : i * 128 + 128]
        s0 = jnp.dot(pick, level2[0], preferred_element_type=F32).astype(BF16)
        s1 = jnp.dot(pick, level2[1], preferred_element_type=F32).astype(BF16)
        own = own + jnp.dot(s0, down2_ref[18 + i], preferred_element_type=F32)
        nxt = nxt + jnp.dot(s0, down2_ref[i], preferred_element_type=F32)
        nxt = nxt + jnp.dot(s1, down2_ref[9 + i], preferred_element_type=F32)
        lhs2[0, 0:128, i * 128 : i * 128 + 128] = s0[:, 0:128]
        lhs2[1, 0:128, i * 128 : i * 128 + 128] = s0[:, 128:256]
    next2[...] = nxt
    part2_copy = to_right(next2, part2, 3)
    send(part2_copy)
    own2[...] = own

    @pl.when(me == 0)
    def _():
        extra = jnp.zeros((128, 256), F32)
        for i in range(9):
            s0 = jnp.concatenate(
                [lhs2[0, 0:128, i * 128 : i * 128 + 128], lhs2[1, 0:128, i * 128 : i * 128 + 128]], axis=1
            )
            extra = extra + jnp.dot(s0, down2_ref[i], preferred_element_type=F32)
            extra = extra + jnp.dot(s0, down2_ref[9 + i], preferred_element_type=F32)
        part2[...] = extra

    landed(part2_copy)
    enc[...] = (own2[...] + part2[...]).astype(BF16)
    swap = pltpu.make_async_remote_copy(
        src_ref=enc,
        dst_ref=renc,
        send_sem=sems.at[8],
        recv_sem=sems.at[9],
        device_id={"tile": partner},
        device_id_type=MESH,
    )
    swap.start()
    out_ref[0] = enc[...]
    sent(lhalo_copy)
    sent(part2_copy)
    swap.wait()
    out_ref[1] = renc[...]


def encode(xa, xb, sums, params, n):
    (
        first_gain,
        first_shift,
        first_conv,
        first_down,
        second_gain,
        second_shift,
        second_conv,
        second_short,
        second_down,
    ) = params
    cells = xa.shape[2:]
    rows = OWN * 64
    vm = pltpu.VMEM
    line = lambda v: v.reshape(1, 128)
    return pl.pallas_call(
        functools.partial(main_kernel, n, float(cells[0] * cells[1] * (cells[2] // GROUPS))),
        out_shape=jax.ShapeDtypeStruct((2, OWN * 16, 256), BF16),
        in_specs=[VMEM] * 13,
        out_specs=VMEM,
        scratch_shapes=[
            vm((2, 2 * OWN, 128), F32),
            vm((n, 2, 2 * OWN, 128), F32),
            vm((2, 2 * OWN, 128), F32),
            vm((n, 2, 2 * OWN, 128), F32),
            vm((6, 2, OWN, 128), F32),
            vm((4, 2, OWN, 128), F32),
            vm((2, OWN) + cells, BF16),
            vm((2, 288, 768), BF16),
            vm((6, 768, 256), BF16),
            vm((3, 768, 256), BF16),
            vm((2, 256, 128), F32),
            vm((3, rows, 768), BF16),
            vm((rows, 128), F32),
            vm((rows, 128), F32),
            vm((rows, 128), F32),
            vm((2, rows, 128), BF16),
            vm((2, rows, 128), BF16),
            vm((4, rows, 1152), BF16),
            vm((OWN * 16, 256), F32),
            vm((OWN * 16, 256), F32),
            vm((OWN * 16, 256), F32),
            vm((OWN * 16, 256), BF16),
            vm((OWN * 16, 256), BF16),
            pltpu.SemaphoreType.DMA((n,)),
            pltpu.SemaphoreType.DMA((n,)),
            pltpu.SemaphoreType.DMA((n,)),
            pltpu.SemaphoreType.DMA((n,)),
            pltpu.SemaphoreType.DMA((10,)),
        ],
        name="encode",
        compiler_params=pltpu.CompilerParams(collective_id=0, has_side_effects=True, vmem_limit_bytes=LIMIT),
    )(
        xa,
        xb,
        sums,
        line(first_gain),
        line(first_shift),
        first_conv,
        first_down,
        line(second_gain),
        line(second_shift),
        second_conv.reshape(3, 1152, 256),
        second_short,
        second_down.reshape(27, 256, 256),
        jnp.asarray(pick_matrix(), BF16),
    )


def swapped(value):
    return lax.ppermute(value, "tile", [(0, 1), (1, 0)])


def body(
    activations,
    tile_ids,
    tile_counts,
    first_gain,
    first_shift,
    first_conv,
    first_down,
    second_gain,
    second_shift,
    second_conv,
    second_short,
    second_down,
):
    n = lax.axis_size("tm")
    me = lax.axis_index("tile")
    cap = activations.shape[1]
    recv = swapped(activations[:, OWN:cap])
    info = jnp.concatenate([tile_ids, tile_counts])
    other = swapped(info)
    heavy = (tile_counts[0] == cap).astype(jnp.int32).reshape(1)

    def encoded_ids(a, b):
        slots = jnp.arange(cap)
        ids_a = jnp.where(slots < a[cap], a[:cap], -1)
        ids_b = jnp.where(slots < b[cap], b[:cap], -1)
        kept = jnp.where(a[cap] == cap, ids_a[OWN - MOVED : OWN], ids_b[OWN:])
        return jnp.concatenate([ids_a[: OWN - MOVED], kept])

    ids = jnp.concatenate([encoded_ids(info, other), encoded_ids(other, info)])

    xa, xb, sums = prep(activations, recv, heavy)
    params = (
        first_gain,
        first_shift,
        first_conv,
        first_down,
        second_gain,
        second_shift,
        second_conv,
        second_short,
        second_down,
    )
    both = encode(xa, xb, sums, params, n).reshape(2 * OWN, 16 * 256)
    select = (ids[None, :] == (me * OWN + jnp.arange(OWN))[:, None]).astype(BF16)
    latents = jnp.dot(select, both, preferred_element_type=F32).astype(BF16)
    return latents.reshape(1, OWN, 4, 4, 256)


def solution(mesh):
    placed = (
        P(("groups", "tm"), "tile", None, None, None),
        P(("groups", "tile")),
        P(("groups", "tile")),
    ) + (P(),) * 9
    return jax.shard_map(
        body,
        mesh=mesh,
        in_specs=placed,
        out_specs=P(("groups", "tm"), "tile", None, None, None),
        check_vma=False,
    )
```

```python
import functools

import jax
import jax.numpy as jnp
import numpy as np
from jax import lax
from jax.experimental import pallas as pl
from jax.experimental.pallas import tpu as pltpu
from jax.sharding import PartitionSpec as P

GROUPS = 32
OWN = 8
MOVED = 4
EPS = 1e-06
F32 = jnp.float32
BF16 = jnp.bfloat16
MESH = pl.DeviceIdType.MESH
VMEM = pl.BlockSpec(memory_space=pltpu.VMEM)
ANY = pl.BlockSpec(memory_space=pl.ANY)
LIMIT = 56 << 20


def silu(u):
    return (0.5 * u) * (1.0 + jnp.tanh(0.5 * u))


def shifted(v, side):
    rows = v.shape[0]
    col = lax.broadcasted_iota(jnp.int32, v.shape, 0) % side
    left = jnp.where(col == 0, 0.0, pltpu.roll(v, 1, axis=0))
    right = jnp.where(col == side - 1, 0.0, pltpu.roll(v, rows - 1, axis=0))
    return left, right


def pick_matrix():
    m = np.zeros((9, OWN, 4, 4, OWN, 8, 8), np.float32)
    for b in range(3):
        for c in range(3):
            for y in range(4):
                for x in range(4):
                    h, w = 2 * y + b - 1, 2 * x + c - 1
                    if 0 <= h < 8 and 0 <= w < 8:
                        for t in range(OWN):
                            m[b * 3 + c, t, y, x, t, h, w] = 1.0
    return m.reshape(9 * OWN * 16, OWN * 64)


def main_kernel(
    n,
    per_frame,
    act_ref,
    info_ref,
    gain1_ref,
    shift1_ref,
    conv1_ref,
    down1_ref,
    gain2_ref,
    shift2_ref,
    conv2_hbm,
    short_ref,
    down2_hbm,
    pick_hbm,
    out_ref,
    x,
    moved,
    rinfo,
    s_ref,
    conv2_ref,
    down2_ref,
    pick_ref,
    mine1,
    got1,
    mine2,
    got2,
    p1,
    p2,
    halo,
    buf,
    w2,
    wd,
    sf,
    lhs,
    own1,
    next1,
    part1,
    level,
    lhalo,
    lhs2,
    own2,
    next2,
    part2,
    enc,
    renc,
    send1,
    recv1,
    send2,
    recv2,
    sems,
    hsend,
    hrecv,
    local,
):
    me = lax.axis_index("tm")
    right = lax.rem(me + 1, n)
    fetch = pltpu.make_async_copy(act_ref.at[:, 0:OWN], x, local.at[0])
    fetch.start()
    partner = 1 - lax.axis_index("tile")
    barrier = pltpu.get_barrier_semaphore()
    for k in range(1, n):
        pl.semaphore_signal(barrier, inc=1, device_id={"tm": lax.rem(me + k, n)}, device_id_type=MESH)
    pl.semaphore_signal(barrier, inc=1, device_id={"tile": partner}, device_id_type=MESH)

    def to_right(src, dst, i):
        return pltpu.make_async_remote_copy(
            src_ref=src,
            dst_ref=dst,
            send_sem=sems.at[2 * i],
            recv_sem=sems.at[2 * i + 1],
            device_id={"tm": right},
            device_id_type=MESH,
        )

    def send(copy):
        @pl.when(me < n - 1)
        def _():
            copy.start()

    def sent(copy):
        @pl.when(me < n - 1)
        def _():
            copy.wait_send()

    def landed(copy):
        @pl.when(me > 0)
        def _():
            copy.wait_recv()

    def fill(sums, mine):
        partial = sums[0]
        for f in range(1, len(sums) - 1):
            partial = partial + sums[f]
        mine[1] = partial
        mine[0] = partial + sums[-1]

    def share(mine, got, send_sem, recv_sem):
        copies = []
        for k in range(1, n):
            src, dst = (mine, got.at[k]) if k == 1 else (mine.at[0], got.at[k, 0])
            c = pltpu.make_async_remote_copy(
                src_ref=src,
                dst_ref=dst,
                send_sem=send_sem.at[k],
                recv_sem=recv_sem.at[k],
                device_id={"tm": lax.rem(me + k, n)},
                device_id_type=MESH,
            )
            c.start()
            copies.append(c)
        return copies

    def norms(sums, copies, got, gain, size, out):
        frames = len(sums)
        rest = jnp.zeros_like(sums[0])
        for k in range(n - 1, 1, -1):
            copies[k - 1].wait()
            rest = rest + jnp.where(k <= me, got[k, 0], 0.0)
        copies[0].wait()
        before = rest + jnp.where(me >= 1, got[1, 0], 0.0)
        rows = [rest + jnp.where(me >= 1, got[1, 1], 0.0), before]
        run = before
        for f in range(frames):
            run = run + sums[f]
            rows.append(run)
        ri = lax.broadcasted_iota(jnp.int32, (128, 128), 0) // (128 // GROUPS)
        ci = lax.broadcasted_iota(jnp.int32, (128, 128), 1) // (128 // GROUPS)
        same = jnp.where(ri == ci, 1.0, 0.0).astype(F32)
        grouped = jnp.dot(
            jnp.concatenate(rows, axis=0), same, precision=lax.Precision.HIGHEST, preferred_element_type=F32
        )
        start = (me * frames).astype(F32)
        made = []
        for i in range(frames + 2):
            count = jnp.maximum(start + float(i - 1), 1.0) * size
            inv_count = jnp.full((1, 128), 1.0, F32) / (jnp.zeros((1, 128), F32) + count)
            g = grouped[i * 2 * OWN : (i + 1) * 2 * OWN]
            m = g[0:OWN] * inv_count
            var = g[OWN : 2 * OWN] * inv_count - m * m
            made.append((m, lax.rsqrt(var + EPS) * gain[...]))
        for i in range(frames + 2):
            for z in range(2):
                v = made[i][z]
                out[i, z] = jnp.where(me == 0, made[2][z], v) if i < 2 else v

    pl.semaphore_wait(barrier, n)

    def swap(src, dst, i):
        return pltpu.make_async_remote_copy(
            src_ref=src,
            dst_ref=dst,
            send_sem=sems.at[2 * i],
            recv_sem=sems.at[2 * i + 1],
            device_id={"tile": partner},
            device_id_type=MESH,
        )

    move_copy = swap(act_ref.at[:, OWN : OWN + MOVED], moved, 5)
    move_copy.start()
    info_copy = swap(info_ref, rinfo, 6)
    info_copy.start()
    late = [
        pltpu.make_async_copy(a, b, local.at[1 + i])
        for i, (a, b) in enumerate(((conv2_hbm, conv2_ref), (down2_hbm, down2_ref), (pick_hbm, pick_ref)))
    ]
    zero = jnp.zeros((128, 128), BF16)
    for q in range(4):
        for b in range(3):
            for c in range(3):
                for e in range(2):
                    a = q - e
                    k = (q % 2) * 384 + c * 128
                    w2[(q // 2) * 3 + b, k : k + 128, e * 128 : e * 128 + 128] = (
                        conv1_ref[a, b, c] if 0 <= a < 3 else zero
                    )
    for b in range(3):
        for c in range(3):
            wd[b, c * 128 : c * 128 + 128, 0:128] = down1_ref[2, b, c]
            wd[b, 384 + c * 128 : 512 + c * 128, 0:128] = zero
            wd[b, c * 128 : c * 128 + 128, 128:256] = down1_ref[0, b, c]
            wd[b, 384 + c * 128 : 512 + c * 128, 128:256] = down1_ref[1, b, c]
    edge = jnp.zeros((16, 768), BF16)
    for z in range(2):
        for p in range(2):
            buf[z, p, 0:16] = edge
            buf[z, p, 272:288] = edge

    heavy = info_ref[2:3, :] == 1

    def add_up(f, j, v):
        s_ref[f, pl.ds(j, 1), :] = jnp.sum(v, axis=0, keepdims=True)
        s_ref[f, pl.ds(OWN + j, 1), :] = jnp.sum(v * v, axis=0, keepdims=True)

    fetch.wait()

    def count_own(j, _):
        for f in range(4):
            add_up(f, j, x[f, j].astype(F32).reshape(256, 128))
        return 0

    lax.fori_loop(0, OWN - MOVED, count_own, 0)
    move_copy.wait()

    def count_moved(i, _):
        j = OWN - MOVED + i
        for f in range(4):
            a = x[f, j].astype(F32).reshape(256, 128)
            v = jnp.where(heavy, a, moved[f, i].astype(F32).reshape(256, 128))
            x[f, j] = v.astype(BF16).reshape(x.shape[2:])
            add_up(f, j, v)
        return 0

    lax.fori_loop(0, MOVED, count_moved, 0)
    for c in late:
        c.start()
    sums1 = [s_ref[f] for f in range(4)]
    fill(sums1, mine1)
    copies1 = share(mine1, got1, send1, recv1)
    norms(sums1, copies1, got1, gain1_ref, per_frame, p1)

    def halo_copy(j):
        return pltpu.make_async_remote_copy(
            src_ref=x.at[2:4, j],
            dst_ref=halo.at[:, j],
            send_sem=hsend.at[j],
            recv_sem=hrecv.at[j],
            device_id={"tm": right},
            device_id_type=MESH,
        )

    @pl.when(me < n - 1)
    def _():
        for j in range(OWN):
            halo_copy(j).start()

    def first_tiles(base, ready):
        def frame(q, j):
            if base == 2:
                return x[q, j]
            return halo[q, j] if q < 2 else x[q - 2, j]

        def prep(j, z):
            for q in range(4):
                v = frame(q, j).astype(F32).reshape(256, 128)
                mean = p1[base + q, 0, pl.ds(j, 1), :]
                scale = p1[base + q, 1, pl.ds(j, 1), :]
                h = silu((v - mean) * scale + shift1_ref[...])
                left, right_ = shifted(h, 16)
                k = (q % 2) * 384
                buf[z, q // 2, 16:272, k : k + 128] = left.astype(BF16)
                buf[z, q // 2, 16:272, k + 128 : k + 256] = h.astype(BF16)
                buf[z, q // 2, 16:272, k + 256 : k + 384] = right_.astype(BF16)

        def multiply(j, z):
            acc = jnp.zeros((256, 256), F32)
            for p in range(2):
                for b in range(3):
                    acc = acc + jnp.dot(
                        buf[z, p, b * 16 : b * 16 + 256, :], w2[p * 3 + b], preferred_element_type=F32
                    )
            for e in range(2):
                v = frame(2 + e, j).astype(F32).reshape(256, 128)
                sf[z, e] = (v + acc[:, e * 128 : e * 128 + 128]).astype(BF16).astype(F32)
            row = pl.multiple_of(j * 64, 64)
            col = lax.broadcasted_iota(jnp.int32, (128, 128), 0) % 8
            for e in range(2):
                even = sf[z, e, pl.ds(0, 128, stride=2), :]
                odd = sf[z, e, pl.ds(1, 128, stride=2), :]
                prev = jnp.where(col == 0, 0.0, pltpu.roll(odd, 1, axis=0))
                for c, v in enumerate((prev, even, odd)):
                    v = v.reshape(8, 2, 8, 128)
                    top, low = v[:, 0], v[:, 1]
                    up = jnp.concatenate([jnp.zeros((1, 8, 128), F32), low[:7]], axis=0)
                    k = e * 384 + c * 128
                    for b, u in enumerate((up, top, low)):
                        lhs[b, pl.ds(row, 64), k : k + 128] = u.reshape(64, 128).astype(BF16)

        def step(i, _):
            ready(2 * i + 1, True)
            ready(2 * i + 2, i < OWN // 2 - 1)
            prep(2 * i + 1, 1)
            multiply(2 * i, 0)
            prep(jnp.minimum(2 * i + 2, OWN - 1), 0)
            multiply(2 * i + 1, 1)
            return 0

        ready(0, True)
        prep(0, 0)
        lax.fori_loop(0, OWN // 2, step, 0)
        out = jnp.zeros((512, 256), F32)
        for b in range(3):
            out = out + jnp.dot(lhs[b], wd[b], preferred_element_type=F32)
        return out

    out = first_tiles(2, lambda j, some: None)
    own1[...] = out[:, 0:128]
    next1[...] = out[:, 128:256]
    part_copy = to_right(next1, part1, 1)
    send(part_copy)

    @pl.when(me == 0)
    def _():
        halo[0] = x[0]
        halo[1] = x[0]

    def halo_ready(j, some):
        @pl.when(jnp.logical_and(me > 0, some))
        def _():
            halo_copy(j).wait_recv()

    out = first_tiles(0, halo_ready)
    level[1] = (own1[...] + out[:, 128:256]).astype(BF16)
    own1[...] = out[:, 0:128]

    @pl.when(me == 0)
    def _():
        extra = jnp.zeros((512, 128), F32)
        for b in range(3):
            twice = jnp.concatenate([lhs[b, :, 0:384], lhs[b, :, 0:384]], axis=1)
            extra = extra + jnp.dot(twice, wd[b, :, 128:256], preferred_element_type=F32)
        part1[...] = extra

    landed(part_copy)
    level[0] = (own1[...] + part1[...]).astype(BF16)

    @pl.when(me < n - 1)
    def _():
        for j in range(OWN):
            halo_copy(j).wait_send()

    sent(part_copy)

    sums2 = []
    for f in range(2):
        v = level[f].astype(F32).reshape(OWN, 64, 128)
        sums2.append(jnp.concatenate([jnp.sum(v, axis=1), jnp.sum(v * v, axis=1)], axis=0))
    fill(sums2, mine2)
    copies2 = share(mine2, got2, send2, recv2)
    lhalo_copy = to_right(level, lhalo, 2)
    send(lhalo_copy)

    @pl.when(me == 0)
    def _():
        lhalo[0] = level[0]
        lhalo[1] = level[0]

    norms(sums2, copies2, got2, gain2_ref, per_frame / 4, p2)

    def second_tiles(base, ref):
        def step(t, _):
            rows = pl.ds(pl.multiple_of(t * 64, 64), 64)
            for q in range(2):
                v = ref[q, rows, :].astype(F32)
                mean = p2[base + q, 0, pl.ds(t, 1), :]
                scale = p2[base + q, 1, pl.ds(t, 1), :]
                h = silu((v - mean) * scale + shift2_ref[...])
                left, right_ = shifted(h, 8)
                pad = jnp.zeros((8, 128), F32)
                for c, v in enumerate((left, h, right_)):
                    up = jnp.concatenate([pad, v[:56]], axis=0)
                    low = jnp.concatenate([v[8:], pad], axis=0)
                    for b, u in enumerate((up, v, low)):
                        k = (b * 3 + c) * 128
                        lhs2[base + q, rows, k : k + 128] = u.astype(BF16)
            return 0

        lax.fori_loop(0, OWN, step, 0)

    second_tiles(2, level)
    landed(lhalo_copy)
    second_tiles(0, lhalo)
    late[0].wait()
    level2 = []
    for f in range(2):
        acc = jnp.dot(level[f], short_ref[...], preferred_element_type=F32)
        for a in range(3):
            acc = acc + jnp.dot(lhs2[f + a], conv2_ref[a], preferred_element_type=F32)
        level2.append(acc.astype(BF16))
    late[1].wait()
    late[2].wait()
    own = jnp.zeros((128, 256), F32)
    nxt = jnp.zeros((128, 256), F32)
    for i in range(9):
        pick = pick_ref[i * 128 : i * 128 + 128]
        s0 = jnp.dot(pick, level2[0], preferred_element_type=F32).astype(BF16)
        s1 = jnp.dot(pick, level2[1], preferred_element_type=F32).astype(BF16)
        own = own + jnp.dot(s0, down2_ref[18 + i], preferred_element_type=F32)
        nxt = nxt + jnp.dot(s0, down2_ref[i], preferred_element_type=F32)
        nxt = nxt + jnp.dot(s1, down2_ref[9 + i], preferred_element_type=F32)
        lhs2[0, 0:128, i * 128 : i * 128 + 128] = s0[:, 0:128]
        lhs2[1, 0:128, i * 128 : i * 128 + 128] = s0[:, 128:256]
    next2[...] = nxt
    part2_copy = to_right(next2, part2, 3)
    send(part2_copy)
    own2[...] = own

    @pl.when(me == 0)
    def _():
        extra = jnp.zeros((128, 256), F32)
        for i in range(9):
            s0 = jnp.concatenate(
                [lhs2[0, 0:128, i * 128 : i * 128 + 128], lhs2[1, 0:128, i * 128 : i * 128 + 128]], axis=1
            )
            extra = extra + jnp.dot(s0, down2_ref[i], preferred_element_type=F32)
            extra = extra + jnp.dot(s0, down2_ref[9 + i], preferred_element_type=F32)
        part2[...] = extra

    landed(part2_copy)
    enc[...] = (own2[...] + part2[...]).astype(BF16)
    enc_copy = swap(enc, renc, 4)
    enc_copy.start()
    info_copy.wait()
    lane = lax.broadcasted_iota(jnp.int32, (1, 128), 1)
    low = lane < (OWN - MOVED) * 16
    my_ids = jnp.where(low | heavy, info_ref[0:1, :], rinfo[1:2, :])
    its_ids = jnp.where(low | (rinfo[2:3, :] == 1), rinfo[0:1, :], info_ref[1:2, :])
    row = lax.broadcasted_iota(jnp.int32, (128, 128), 0)
    wanted = lax.axis_index("tile") * OWN + row // 16
    cell = row % 16 == lax.broadcasted_iota(jnp.int32, (128, 128), 1) % 16
    mine = jnp.where((wanted == my_ids) & cell, 1.0, 0.0).astype(BF16)
    its = jnp.where((wanted == its_ids) & cell, 1.0, 0.0).astype(BF16)
    kept = jnp.dot(mine, enc[...], preferred_element_type=F32)
    sent(lhalo_copy)
    sent(part2_copy)
    enc_copy.wait()
    out_ref[...] = (kept + jnp.dot(its, renc[...], preferred_element_type=F32)).astype(BF16)


def encode(acts, info, params, n):
    (
        first_gain,
        first_shift,
        first_conv,
        first_down,
        second_gain,
        second_shift,
        second_conv,
        second_short,
        second_down,
    ) = params
    cells = acts.shape[2:]
    rows = OWN * 64
    vm = pltpu.VMEM
    line = lambda v: v.reshape(1, 128)
    return pl.pallas_call(
        functools.partial(main_kernel, n, float(cells[0] * cells[1] * (cells[2] // GROUPS))),
        out_shape=jax.ShapeDtypeStruct((OWN * 16, 256), BF16),
        in_specs=[ANY] + [VMEM] * 7 + [ANY, VMEM, ANY, ANY],
        out_specs=VMEM,
        scratch_shapes=[
            vm((4, OWN) + cells, BF16),
            vm((4, MOVED) + cells, BF16),
            vm((8, 128), jnp.int32),
            vm((4, 2 * OWN, 128), F32),
            vm((3, 1152, 256), BF16),
            vm((27, 256, 256), BF16),
            vm((9 * OWN * 16, rows), BF16),
            vm((2, 2 * OWN, 128), F32),
            vm((n, 2, 2 * OWN, 128), F32),
            vm((2, 2 * OWN, 128), F32),
            vm((n, 2, 2 * OWN, 128), F32),
            vm((6, 2, OWN, 128), F32),
            vm((4, 2, OWN, 128), F32),
            vm((2, OWN) + cells, BF16),
            vm((2, 2, 288, 768), BF16),
            vm((6, 768, 256), BF16),
            vm((3, 768, 256), BF16),
            vm((2, 2, 256, 128), F32),
            vm((3, rows, 768), BF16),
            vm((rows, 128), F32),
            vm((rows, 128), F32),
            vm((rows, 128), F32),
            vm((2, rows, 128), BF16),
            vm((2, rows, 128), BF16),
            vm((4, rows, 1152), BF16),
            vm((OWN * 16, 256), F32),
            vm((OWN * 16, 256), F32),
            vm((OWN * 16, 256), F32),
            vm((OWN * 16, 256), BF16),
            vm((OWN * 16, 256), BF16),
            pltpu.SemaphoreType.DMA((n,)),
            pltpu.SemaphoreType.DMA((n,)),
            pltpu.SemaphoreType.DMA((n,)),
            pltpu.SemaphoreType.DMA((n,)),
            pltpu.SemaphoreType.DMA((14,)),
            pltpu.SemaphoreType.DMA((OWN,)),
            pltpu.SemaphoreType.DMA((OWN,)),
            pltpu.SemaphoreType.DMA((4,)),
        ],
        name="encode",
        compiler_params=pltpu.CompilerParams(collective_id=0, has_side_effects=True, vmem_limit_bytes=LIMIT),
    )(
        acts,
        info,
        line(first_gain),
        line(first_shift),
        first_conv,
        first_down,
        line(second_gain),
        line(second_shift),
        second_conv.reshape(3, 1152, 256),
        second_short,
        second_down.reshape(27, 256, 256),
        jnp.asarray(pick_matrix(), BF16),
    )


def body(
    activations,
    tile_ids,
    tile_counts,
    first_gain,
    first_shift,
    first_conv,
    first_down,
    second_gain,
    second_shift,
    second_conv,
    second_short,
    second_down,
):
    n = lax.axis_size("tm")
    cap = activations.shape[1]
    count = tile_counts[0]
    ids = jnp.repeat(jnp.where(jnp.arange(cap) < count, tile_ids, -1), 16)
    split = (OWN - MOVED) * 16
    kept = ids[: OWN * 16]
    mixed = jnp.concatenate([ids[:split], ids[OWN * 16 :]])
    heavy = jnp.full((OWN * 16,), count == cap, jnp.int32)
    info = jnp.stack([kept, mixed] + [heavy] * 6)
    params = (
        first_gain,
        first_shift,
        first_conv,
        first_down,
        second_gain,
        second_shift,
        second_conv,
        second_short,
        second_down,
    )
    latents = encode(activations, info, params, n)
    return latents.reshape(1, OWN, 4, 4, 256)


def solution(mesh):
    placed = (
        P(("groups", "tm"), "tile", None, None, None),
        P(("groups", "tile")),
        P(("groups", "tile")),
    ) + (P(),) * 9
    return jax.shard_map(
        body,
        mesh=mesh,
        in_specs=placed,
        out_specs=P(("groups", "tm"), "tile", None, None, None),
        check_vma=False,
    )
```

```python
import functools

import jax
import jax.numpy as jnp
import numpy as np
from jax import lax
from jax.experimental import pallas as pl
from jax.experimental.pallas import tpu as pltpu
from jax.sharding import PartitionSpec as P

GROUPS = 32
OWN = 8
MOVED = 4
EPS = 1e-06
F32 = jnp.float32
BF16 = jnp.bfloat16
MESH = pl.DeviceIdType.MESH
VMEM = pl.BlockSpec(memory_space=pltpu.VMEM)
ANY = pl.BlockSpec(memory_space=pl.ANY)
LIMIT = 56 << 20


def silu(u):
    return (0.5 * u) * (1.0 + jnp.tanh(0.5 * u))


def shifted(v, side):
    rows = v.shape[0]
    col = lax.broadcasted_iota(jnp.int32, v.shape, 0) % side
    left = jnp.where(col == 0, 0.0, pltpu.roll(v, 1, axis=0))
    right = jnp.where(col == side - 1, 0.0, pltpu.roll(v, rows - 1, axis=0))
    return left, right


def pick_matrix():
    m = np.zeros((9, OWN, 4, 4, OWN, 8, 8), np.float32)
    for b in range(3):
        for c in range(3):
            for y in range(4):
                for x in range(4):
                    h, w = 2 * y + b - 1, 2 * x + c - 1
                    if 0 <= h < 8 and 0 <= w < 8:
                        for t in range(OWN):
                            m[b * 3 + c, t, y, x, t, h, w] = 1.0
    return m.reshape(9 * OWN * 16, OWN * 64)


def main_kernel(
    n,
    per_frame,
    act_ref,
    info_ref,
    gain1_ref,
    shift1_ref,
    conv1_ref,
    down1_ref,
    gain2_ref,
    shift2_ref,
    conv2_hbm,
    short_ref,
    down2_hbm,
    pick_hbm,
    out_ref,
    x,
    moved,
    rinfo,
    s_ref,
    conv2_ref,
    down2_ref,
    pick_ref,
    mine1,
    got1,
    mine2,
    got2,
    p1,
    p2,
    halo,
    buf,
    w2,
    wd,
    sf,
    lhs,
    own1,
    next1,
    part1,
    level,
    lhalo,
    lhs2,
    own2,
    next2,
    part2,
    enc,
    renc,
    send1,
    recv1,
    send2,
    recv2,
    sems,
    hsend,
    hrecv,
    local,
):
    me = lax.axis_index("tm")
    right = lax.rem(me + 1, n)
    fetch = pltpu.make_async_copy(act_ref.at[:, 0:OWN], x, local.at[0])
    fetch.start()
    partner = 1 - lax.axis_index("tile")
    barrier = pltpu.get_barrier_semaphore()
    for k in range(1, n):
        pl.semaphore_signal(barrier, inc=1, device_id={"tm": lax.rem(me + k, n)}, device_id_type=MESH)
    pl.semaphore_signal(barrier, inc=1, device_id={"tile": partner}, device_id_type=MESH)

    def to_right(src, dst, i):
        return pltpu.make_async_remote_copy(
            src_ref=src,
            dst_ref=dst,
            send_sem=sems.at[2 * i],
            recv_sem=sems.at[2 * i + 1],
            device_id={"tm": right},
            device_id_type=MESH,
        )

    def send(copy):
        @pl.when(me < n - 1)
        def _():
            copy.start()

    def sent(copy):
        @pl.when(me < n - 1)
        def _():
            copy.wait_send()

    def landed(copy):
        @pl.when(me > 0)
        def _():
            copy.wait_recv()

    def fill(sums, mine):
        partial = sums[0]
        for f in range(1, len(sums) - 1):
            partial = partial + sums[f]
        mine[1] = partial
        mine[0] = partial + sums[-1]

    def share(mine, got, send_sem, recv_sem):
        copies = []
        for k in range(1, n):
            src, dst = (mine, got.at[k]) if k == 1 else (mine.at[0], got.at[k, 0])
            c = pltpu.make_async_remote_copy(
                src_ref=src,
                dst_ref=dst,
                send_sem=send_sem.at[k],
                recv_sem=recv_sem.at[k],
                device_id={"tm": lax.rem(me + k, n)},
                device_id_type=MESH,
            )
            c.start()
            copies.append(c)
        return copies

    def norms(sums, copies, got, gain, size, out):
        frames = len(sums)
        rest = jnp.zeros_like(sums[0])
        for k in range(n - 1, 1, -1):
            copies[k - 1].wait()
            rest = rest + jnp.where(k <= me, got[k, 0], 0.0)
        copies[0].wait()
        before = rest + jnp.where(me >= 1, got[1, 0], 0.0)
        rows = [rest + jnp.where(me >= 1, got[1, 1], 0.0), before]
        run = before
        for f in range(frames):
            run = run + sums[f]
            rows.append(run)
        ri = lax.broadcasted_iota(jnp.int32, (128, 128), 0) // (128 // GROUPS)
        ci = lax.broadcasted_iota(jnp.int32, (128, 128), 1) // (128 // GROUPS)
        same = jnp.where(ri == ci, 1.0, 0.0).astype(F32)
        grouped = jnp.dot(
            jnp.concatenate(rows, axis=0), same, precision=lax.Precision.HIGHEST, preferred_element_type=F32
        )
        start = (me * frames).astype(F32)
        made = []
        for i in range(frames + 2):
            count = jnp.maximum(start + float(i - 1), 1.0) * size
            inv_count = jnp.full((1, 128), 1.0, F32) / (jnp.zeros((1, 128), F32) + count)
            g = grouped[i * 2 * OWN : (i + 1) * 2 * OWN]
            m = g[0:OWN] * inv_count
            var = g[OWN : 2 * OWN] * inv_count - m * m
            made.append((m, lax.rsqrt(var + EPS) * gain[...]))
        for i in range(frames + 2):
            for z in range(2):
                v = made[i][z]
                out[i, z] = jnp.where(me == 0, made[2][z], v) if i < 2 else v

    pl.semaphore_wait(barrier, n)

    def swap(src, dst, i):
        return pltpu.make_async_remote_copy(
            src_ref=src,
            dst_ref=dst,
            send_sem=sems.at[2 * i],
            recv_sem=sems.at[2 * i + 1],
            device_id={"tile": partner},
            device_id_type=MESH,
        )

    move_copy = swap(act_ref.at[:, OWN : OWN + MOVED], moved, 5)
    move_copy.start()
    info_copy = swap(info_ref, rinfo, 6)
    info_copy.start()
    late = [
        pltpu.make_async_copy(a, b, local.at[1 + i])
        for i, (a, b) in enumerate(((conv2_hbm, conv2_ref), (down2_hbm, down2_ref), (pick_hbm, pick_ref)))
    ]
    zero = jnp.zeros((128, 128), BF16)
    for q in range(4):
        for b in range(3):
            for c in range(3):
                for e in range(2):
                    a = q - e
                    k = (q % 2) * 384 + c * 128
                    w2[(q // 2) * 3 + b, k : k + 128, e * 128 : e * 128 + 128] = (
                        conv1_ref[a, b, c] if 0 <= a < 3 else zero
                    )
    for b in range(3):
        for c in range(3):
            wd[b, c * 128 : c * 128 + 128, 0:128] = down1_ref[2, b, c]
            wd[b, 384 + c * 128 : 512 + c * 128, 0:128] = zero
            wd[b, c * 128 : c * 128 + 128, 128:256] = down1_ref[0, b, c]
            wd[b, 384 + c * 128 : 512 + c * 128, 128:256] = down1_ref[1, b, c]
    edge = jnp.zeros((16, 768), BF16)
    for z in range(2):
        for p in range(2):
            buf[z, p, 0:16] = edge
            buf[z, p, 272:288] = edge

    heavy = info_ref[2:3, :] == 1

    def add_up(f, j, v):
        s_ref[f, pl.ds(j, 1), :] = jnp.sum(v, axis=0, keepdims=True)
        s_ref[f, pl.ds(OWN + j, 1), :] = jnp.sum(v * v, axis=0, keepdims=True)

    fetch.wait()

    def count_own(j, _):
        for f in range(4):
            add_up(f, j, x[f, j].astype(F32).reshape(256, 128))
        return 0

    lax.fori_loop(0, OWN - MOVED, count_own, 0)
    move_copy.wait()

    def count_moved(i, _):
        j = OWN - MOVED + i
        for f in range(4):
            a = x[f, j].astype(F32).reshape(256, 128)
            v = jnp.where(heavy, a, moved[f, i].astype(F32).reshape(256, 128))
            x[f, j] = v.astype(BF16).reshape(x.shape[2:])
            add_up(f, j, v)
        return 0

    lax.fori_loop(0, MOVED, count_moved, 0)
    for c in late:
        c.start()
    sums1 = [s_ref[f] for f in range(4)]
    fill(sums1, mine1)
    copies1 = share(mine1, got1, send1, recv1)
    def halo_copy(j):
        return pltpu.make_async_remote_copy(
            src_ref=x.at[2:4, j],
            dst_ref=halo.at[:, j],
            send_sem=hsend.at[j],
            recv_sem=hrecv.at[j],
            device_id={"tm": right},
            device_id_type=MESH,
        )

    @pl.when(me < n - 1)
    def _():
        for j in range(OWN):
            halo_copy(j).start()

    norms(sums1, copies1, got1, gain1_ref, per_frame, p1)

    def first_tiles(base, ready):
        def frame(q, j):
            if base == 2:
                return x[q, j]
            return halo[q, j] if q < 2 else x[q - 2, j]

        def prep(j, z):
            for q in range(4):
                v = frame(q, j).astype(F32).reshape(256, 128)
                mean = p1[base + q, 0, pl.ds(j, 1), :]
                scale = p1[base + q, 1, pl.ds(j, 1), :]
                h = silu((v - mean) * scale + shift1_ref[...])
                left, right_ = shifted(h, 16)
                k = (q % 2) * 384
                buf[z, q // 2, 16:272, k : k + 128] = left.astype(BF16)
                buf[z, q // 2, 16:272, k + 128 : k + 256] = h.astype(BF16)
                buf[z, q // 2, 16:272, k + 256 : k + 384] = right_.astype(BF16)

        def multiply(j, z):
            acc = jnp.zeros((256, 256), F32)
            for p in range(2):
                for b in range(3):
                    acc = acc + jnp.dot(
                        buf[z, p, b * 16 : b * 16 + 256, :], w2[p * 3 + b], preferred_element_type=F32
                    )
            for e in range(2):
                v = frame(2 + e, j).astype(F32).reshape(256, 128)
                sf[z, e] = (v + acc[:, e * 128 : e * 128 + 128]).astype(BF16).astype(F32)
            row = pl.multiple_of(j * 64, 64)
            col = lax.broadcasted_iota(jnp.int32, (128, 128), 0) % 8
            for e in range(2):
                even = sf[z, e, pl.ds(0, 128, stride=2), :]
                odd = sf[z, e, pl.ds(1, 128, stride=2), :]
                prev = jnp.where(col == 0, 0.0, pltpu.roll(odd, 1, axis=0))
                for c, v in enumerate((prev, even, odd)):
                    v = v.reshape(8, 2, 8, 128)
                    top, low = v[:, 0], v[:, 1]
                    up = jnp.concatenate([jnp.zeros((1, 8, 128), F32), low[:7]], axis=0)
                    k = e * 384 + c * 128
                    for b, u in enumerate((up, top, low)):
                        lhs[b, pl.ds(row, 64), k : k + 128] = u.reshape(64, 128).astype(BF16)

        def step(i, _):
            ready(2 * i + 1, True)
            ready(2 * i + 2, i < OWN // 2 - 1)
            prep(2 * i + 1, 1)
            multiply(2 * i, 0)
            prep(jnp.minimum(2 * i + 2, OWN - 1), 0)
            multiply(2 * i + 1, 1)
            return 0

        ready(0, True)
        prep(0, 0)
        lax.fori_loop(0, OWN // 2, step, 0)
        out = jnp.zeros((512, 256), F32)
        for b in range(3):
            out = out + jnp.dot(lhs[b], wd[b], preferred_element_type=F32)
        return out

    out = first_tiles(2, lambda j, some: None)
    own1[...] = out[:, 0:128]
    next1[...] = out[:, 128:256]
    part_copy = to_right(next1, part1, 1)
    send(part_copy)

    @pl.when(me == 0)
    def _():
        halo[0] = x[0]
        halo[1] = x[0]

    def halo_ready(j, some):
        @pl.when(jnp.logical_and(me > 0, some))
        def _():
            halo_copy(j).wait_recv()

    out = first_tiles(0, halo_ready)
    level[1] = (own1[...] + out[:, 128:256]).astype(BF16)
    own1[...] = out[:, 0:128]

    @pl.when(me == 0)
    def _():
        extra = jnp.zeros((512, 128), F32)
        for b in range(3):
            twice = jnp.concatenate([lhs[b, :, 0:384], lhs[b, :, 0:384]], axis=1)
            extra = extra + jnp.dot(twice, wd[b, :, 128:256], preferred_element_type=F32)
        part1[...] = extra

    landed(part_copy)
    level[0] = (own1[...] + part1[...]).astype(BF16)

    @pl.when(me < n - 1)
    def _():
        for j in range(OWN):
            halo_copy(j).wait_send()

    sent(part_copy)

    sums2 = []
    for f in range(2):
        v = level[f].astype(F32).reshape(OWN, 64, 128)
        sums2.append(jnp.concatenate([jnp.sum(v, axis=1), jnp.sum(v * v, axis=1)], axis=0))
    fill(sums2, mine2)
    copies2 = share(mine2, got2, send2, recv2)
    lhalo_copy = to_right(level, lhalo, 2)
    send(lhalo_copy)

    @pl.when(me == 0)
    def _():
        lhalo[0] = level[0]
        lhalo[1] = level[0]

    norms(sums2, copies2, got2, gain2_ref, per_frame / 4, p2)

    def second_tiles(base, ref):
        def step(t, _):
            rows = pl.ds(pl.multiple_of(t * 64, 64), 64)
            for q in range(2):
                v = ref[q, rows, :].astype(F32)
                mean = p2[base + q, 0, pl.ds(t, 1), :]
                scale = p2[base + q, 1, pl.ds(t, 1), :]
                h = silu((v - mean) * scale + shift2_ref[...])
                left, right_ = shifted(h, 8)
                pad = jnp.zeros((8, 128), F32)
                for c, v in enumerate((left, h, right_)):
                    up = jnp.concatenate([pad, v[:56]], axis=0)
                    low = jnp.concatenate([v[8:], pad], axis=0)
                    for b, u in enumerate((up, v, low)):
                        k = (b * 3 + c) * 128
                        lhs2[base + q, rows, k : k + 128] = u.astype(BF16)
            return 0

        lax.fori_loop(0, OWN, step, 0)

    second_tiles(2, level)
    landed(lhalo_copy)
    second_tiles(0, lhalo)
    late[0].wait()
    level2 = []
    for f in range(2):
        acc = jnp.dot(level[f], short_ref[...], preferred_element_type=F32)
        for a in range(3):
            acc = acc + jnp.dot(lhs2[f + a], conv2_ref[a], preferred_element_type=F32)
        level2.append(acc.astype(BF16))
    late[1].wait()
    late[2].wait()
    own = jnp.zeros((128, 256), F32)
    nxt = jnp.zeros((128, 256), F32)
    for i in range(9):
        pick = pick_ref[i * 128 : i * 128 + 128]
        s0 = jnp.dot(pick, level2[0], preferred_element_type=F32).astype(BF16)
        s1 = jnp.dot(pick, level2[1], preferred_element_type=F32).astype(BF16)
        own = own + jnp.dot(s0, down2_ref[18 + i], preferred_element_type=F32)
        nxt = nxt + jnp.dot(s0, down2_ref[i], preferred_element_type=F32)
        nxt = nxt + jnp.dot(s1, down2_ref[9 + i], preferred_element_type=F32)
        lhs2[0, 0:128, i * 128 : i * 128 + 128] = s0[:, 0:128]
        lhs2[1, 0:128, i * 128 : i * 128 + 128] = s0[:, 128:256]
    next2[...] = nxt
    part2_copy = to_right(next2, part2, 3)
    send(part2_copy)
    own2[...] = own

    @pl.when(me == 0)
    def _():
        extra = jnp.zeros((128, 256), F32)
        for i in range(9):
            s0 = jnp.concatenate(
                [lhs2[0, 0:128, i * 128 : i * 128 + 128], lhs2[1, 0:128, i * 128 : i * 128 + 128]], axis=1
            )
            extra = extra + jnp.dot(s0, down2_ref[i], preferred_element_type=F32)
            extra = extra + jnp.dot(s0, down2_ref[9 + i], preferred_element_type=F32)
        part2[...] = extra

    landed(part2_copy)
    enc[...] = (own2[...] + part2[...]).astype(BF16)
    enc_copy = swap(enc, renc, 4)
    enc_copy.start()
    info_copy.wait()
    lane = lax.broadcasted_iota(jnp.int32, (1, 128), 1)
    low = lane < (OWN - MOVED) * 16
    my_ids = jnp.where(low | heavy, info_ref[0:1, :], rinfo[1:2, :])
    its_ids = jnp.where(low | (rinfo[2:3, :] == 1), rinfo[0:1, :], info_ref[1:2, :])
    row = lax.broadcasted_iota(jnp.int32, (128, 128), 0)
    wanted = lax.axis_index("tile") * OWN + row // 16
    cell = row % 16 == lax.broadcasted_iota(jnp.int32, (128, 128), 1) % 16
    mine = jnp.where((wanted == my_ids) & cell, 1.0, 0.0).astype(BF16)
    its = jnp.where((wanted == its_ids) & cell, 1.0, 0.0).astype(BF16)
    kept = jnp.dot(mine, enc[...], preferred_element_type=F32)
    sent(lhalo_copy)
    sent(part2_copy)
    enc_copy.wait()
    out_ref[...] = (kept + jnp.dot(its, renc[...], preferred_element_type=F32)).astype(BF16)


def encode(acts, info, params, n):
    (
        first_gain,
        first_shift,
        first_conv,
        first_down,
        second_gain,
        second_shift,
        second_conv,
        second_short,
        second_down,
    ) = params
    cells = acts.shape[2:]
    rows = OWN * 64
    vm = pltpu.VMEM
    line = lambda v: v.reshape(1, 128)
    return pl.pallas_call(
        functools.partial(main_kernel, n, float(cells[0] * cells[1] * (cells[2] // GROUPS))),
        out_shape=jax.ShapeDtypeStruct((OWN * 16, 256), BF16),
        in_specs=[ANY] + [VMEM] * 7 + [ANY, VMEM, ANY, ANY],
        out_specs=VMEM,
        scratch_shapes=[
            vm((4, OWN) + cells, BF16),
            vm((4, MOVED) + cells, BF16),
            vm((8, 128), jnp.int32),
            vm((4, 2 * OWN, 128), F32),
            vm((3, 1152, 256), BF16),
            vm((27, 256, 256), BF16),
            vm((9 * OWN * 16, rows), BF16),
            vm((2, 2 * OWN, 128), F32),
            vm((n, 2, 2 * OWN, 128), F32),
            vm((2, 2 * OWN, 128), F32),
            vm((n, 2, 2 * OWN, 128), F32),
            vm((6, 2, OWN, 128), F32),
            vm((4, 2, OWN, 128), F32),
            vm((2, OWN) + cells, BF16),
            vm((2, 2, 288, 768), BF16),
            vm((6, 768, 256), BF16),
            vm((3, 768, 256), BF16),
            vm((2, 2, 256, 128), F32),
            vm((3, rows, 768), BF16),
            vm((rows, 128), F32),
            vm((rows, 128), F32),
            vm((rows, 128), F32),
            vm((2, rows, 128), BF16),
            vm((2, rows, 128), BF16),
            vm((4, rows, 1152), BF16),
            vm((OWN * 16, 256), F32),
            vm((OWN * 16, 256), F32),
            vm((OWN * 16, 256), F32),
            vm((OWN * 16, 256), BF16),
            vm((OWN * 16, 256), BF16),
            pltpu.SemaphoreType.DMA((n,)),
            pltpu.SemaphoreType.DMA((n,)),
            pltpu.SemaphoreType.DMA((n,)),
            pltpu.SemaphoreType.DMA((n,)),
            pltpu.SemaphoreType.DMA((14,)),
            pltpu.SemaphoreType.DMA((OWN,)),
            pltpu.SemaphoreType.DMA((OWN,)),
            pltpu.SemaphoreType.DMA((4,)),
        ],
        name="encode",
        compiler_params=pltpu.CompilerParams(collective_id=0, has_side_effects=True, vmem_limit_bytes=LIMIT),
    )(
        acts,
        info,
        line(first_gain),
        line(first_shift),
        first_conv,
        first_down,
        line(second_gain),
        line(second_shift),
        second_conv.reshape(3, 1152, 256),
        second_short,
        second_down.reshape(27, 256, 256),
        jnp.asarray(pick_matrix(), BF16),
    )


def body(
    activations,
    tile_ids,
    tile_counts,
    first_gain,
    first_shift,
    first_conv,
    first_down,
    second_gain,
    second_shift,
    second_conv,
    second_short,
    second_down,
):
    n = lax.axis_size("tm")
    cap = activations.shape[1]
    count = tile_counts[0]
    ids = jnp.repeat(jnp.where(jnp.arange(cap) < count, tile_ids, -1), 16)
    split = (OWN - MOVED) * 16
    kept = ids[: OWN * 16]
    mixed = jnp.concatenate([ids[:split], ids[OWN * 16 :]])
    heavy = jnp.full((OWN * 16,), count == cap, jnp.int32)
    info = jnp.stack([kept, mixed] + [heavy] * 6)
    params = (
        first_gain,
        first_shift,
        first_conv,
        first_down,
        second_gain,
        second_shift,
        second_conv,
        second_short,
        second_down,
    )
    latents = encode(activations, info, params, n)
    return latents.reshape(1, OWN, 4, 4, 256)


def solution(mesh):
    placed = (
        P(("groups", "tm"), "tile", None, None, None),
        P(("groups", "tile")),
        P(("groups", "tile")),
    ) + (P(),) * 9
    return jax.shard_map(
        body,
        mesh=mesh,
        in_specs=placed,
        out_specs=P(("groups", "tm"), "tile", None, None, None),
        check_vma=False,
    )
```
